1024 devices in a mesh: dp: 32 (over y, z_lo), expert: 32 (over x, z_hi, core).
Axes of the slice: x: 8, y: 8, z: 8 (z_hi: 2, z_lo: 4; z = z_hi * 4 + z_lo), core: 2. Of those that a mesh axis runs over, the one named last changes fastest.
Arguments:
- tokens: bfloat16 [512, 7168], P('expert', 'dp'), may hold values from -6 to 6
- routes: int32 [512, 8], P('expert'), may hold values from 0 to 31, all different within a row; in each aligned block of 16 rows (0 to 15, 16 to 31, ...) at most 8 rows name the same one
- scores: float32 [512, 8], P('expert'), may hold values from 0.05 to 1
- w_gate: bfloat16 [32, 7168, 1024], P('expert', 'dp'), may hold values from -0.0625 to 0.0625
- w_up: bfloat16 [32, 7168, 1024], P('expert', 'dp'), may hold values from -0.0625 to 0.0625
- w_down: bfloat16 [32, 7168, 1024], P('expert', 'dp'), may hold values from -0.1875 to 0.1875
- cotangent: bfloat16 [512, 7168], P('expert', 'dp'), may hold values from -6 to 6
Outputs:
- layer_out: bfloat16 [512, 7168], P('expert', 'dp')
- grad_tokens: bfloat16 [512, 7168], P('expert', 'dp')
- grad_gate: bfloat16 [32, 7168, 1024], P('expert', 'dp')
- grad_up: bfloat16 [32, 7168, 1024], P('expert', 'dp')
- grad_down: bfloat16 [32, 7168, 1024], P('expert', 'dp')
The draws below stay inside these ranges and needn't reach their ends.
Inputs may be any that keep to these rules, and one draw needn't show every extreme that they name: `routes`: each row names 8 different experts. In each aligned block of 16 rows (the tokens held by one expert-axis shard) no expert is named by more than 8 rows, a bound that some block reaches.
All inputs are finite; a program needn't handle non-finite values.
Results may differ from the reference program's by a relative error of at most 0.0057.
Values may be sent and summed in bfloat16 or wider, within the bound.
No kernel may reach another device: no remote copies, remote signals or barrier semaphores. Data moves between devices by JAX's collectives and lax.ppermute only.
A program may use at most 32 MiB of HBM per device.

```python
import math
import jax
import jax.numpy as jnp
import numpy as np
from jax import lax

D = 7168
HID = 1024
TOP = 8
EXPERTS = 32
CAP = 8
TOK_DEV = 16
TOKENS = 512


def block_scale(stream_key, shape, split, low, largest):
    gain = 1.0
    for position, parts in split:
        steps = jax.random.uniform(jax.random.fold_in(jax.random.fold_in(stream_key, 6), position), (parts,), jnp.float32, low / len(split), largest / len(split))
        gain = gain * jnp.repeat(jnp.exp(steps), shape[position] // parts).reshape((-1,) + (1,) * (len(shape) - 1 - position))
    return gain


def shared_out(own_key, own, number, rows, number_of, top, most, lean):
    order = jax.random.permutation(own_key, number_of)
    packed, ordinary = shares(number_of, rows * top, most, lean, True), shares(number_of, rows * top, most, lean, False)
    places = jnp.arange(number_of)

    def named(lengths, rotation):
        used = int((lengths > 0).sum())
        fixed = max(1, used // 4)
        moved = fixed + (places - fixed + rotation * (used - fixed)) % max(1, number_of - fixed)
        return jnp.zeros((number_of,), jnp.int32).at[order[jnp.where(places < fixed, places, moved)]].set(jnp.asarray(lengths, jnp.int32))

    lengths = jnp.where(number % 4 == 0, named(packed, number // 4), named(ordinary, number - number // 4 - 1))
    mixed = jax.random.permutation(jax.random.fold_in(own, 3), number_of)
    source_of, taker = mixed[0:number_of // 2 * 2:2], mixed[1:number_of // 2 * 2:2]
    margin = jnp.minimum(lengths[source_of] - 1, most - lengths[taker]) // 2
    margin = jnp.where((source_of == order[0]) | (taker == order[0]) | (lengths[taker] == 0), 0, jnp.maximum(margin, 0))
    moved = jax.random.randint(jax.random.fold_in(own, 4), (number_of // 2,), 0, 1 << 20) % (margin + 1)
    lengths = lengths.at[source_of].add(-moved).at[taker].add(moved)
    members = jnp.searchsorted(jnp.cumsum(lengths), jnp.arange(rows * top), side="right").astype(jnp.int32)
    listing = members.reshape(top, rows).T
    listing = listing[jax.random.permutation(jax.random.fold_in(own, 1), rows)]
    rotation = jax.random.randint(jax.random.fold_in(own, 2), (rows, 1), 0, top)
    return jnp.take_along_axis(listing, (jnp.arange(top)[None, :] + rotation) % top, axis=1)


def shares(number_of, total, limit, slope, full):
    loads = [(1 << 20) // math.isqrt(standing ** slope) + 1 for standing in range(1, number_of + 1)]
    largest = limit if full else min(limit, max(-(-total // number_of), total * loads[0] // sum(loads)))
    least = 1 if total - largest >= number_of - 1 else 0
    given, surplus = [largest] + [least] * (number_of - 1), total - largest - least * (number_of - 1)
    while surplus > 0:
        movable = [i for i in range(1, number_of) if given[i] < largest] or [i for i in range(1, number_of) if given[i] < limit]
        whole, left = sum([loads[i] for i in movable]), surplus
        for i in movable:
            addition = min(limit - given[i], max(1, left * loads[i] // whole), surplus)
            given[i] = given[i] + addition
            surplus = surplus - addition
    return np.array(given)


def bell_draw(own_key, dims, scale, most, cuts=(), kind=jnp.bfloat16):
    gain = block_scale(own_key, dims, cuts, -0.22, 0.18) if cuts else 1.0
    entries = jax.random.normal(own_key, dims, jnp.float32) * scale * gain
    return jnp.minimum(jnp.maximum(entries, -most), most).astype(kind)


def setup_inputs(seed: int = 0) -> dict:
    arg_keys = jax.random.split(jax.random.key(seed), 8)
    tokens = bell_draw(arg_keys[0], (TOKENS, D), 1.0, 6.0, ((0, 32), (1, 32)))
    routes_keys = jax.random.split(jax.random.fold_in(arg_keys[1], 1), TOKENS // TOK_DEV)
    routes_turns = jax.random.permutation(jax.random.fold_in(arg_keys[1], 3), TOKENS // TOK_DEV)
    routes = jax.vmap(lambda own, number: shared_out(jax.random.fold_in(arg_keys[1], 2), own, number, TOK_DEV, EXPERTS, TOP, CAP, 2))(routes_keys, routes_turns).reshape((TOKENS, TOP))
    scores = jnp.clip(jnp.exp(math.log(1.0) - 2.9957323 * jax.random.uniform(arg_keys[2], (TOKENS, TOP), jnp.float32) ** block_scale(arg_keys[2], (TOKENS, TOP), ((0, 32),), -0.2, 0.2)), 0.05, 1.0)
    w_gate = bell_draw(arg_keys[3], (EXPERTS, D, HID), D ** -0.5, 0.0625, ((0, 32), (1, 32)))
    w_up = bell_draw(arg_keys[4], (EXPERTS, D, HID), D ** -0.5, 0.0625, ((0, 32), (1, 32)))
    w_down = bell_draw(arg_keys[5], (EXPERTS, D, HID), HID ** -0.5, 0.1875, ((0, 32), (1, 32)))
    cotangent = bell_draw(arg_keys[6], (TOKENS, D), 1.0, 6.0, ((0, 32), (1, 32)))
    return {"tokens": tokens, "routes": routes, "scores": scores, "w_gate": w_gate, "w_up": w_up, "w_down": w_down, "cotangent": cotangent}


route_scale = 2.5


def expert_pass(rows_x, rows_do, gate_mat, up_mat, down_mat):
    pre_gate = jnp.dot(rows_x, gate_mat, preferred_element_type=jnp.float32)
    pre_up = jnp.dot(rows_x, up_mat, preferred_element_type=jnp.float32)
    sigma = jax.nn.sigmoid(pre_gate)
    active = pre_gate * sigma
    hidden = (active * pre_up).astype(jnp.bfloat16)
    expert_out = jnp.dot(hidden, down_mat.T, preferred_element_type=jnp.float32)
    grad_hidden = jnp.dot(rows_do, down_mat, preferred_element_type=jnp.float32)
    grad_pre_gate = (grad_hidden * pre_up * sigma * (1.0 + pre_gate * (1.0 - sigma))).astype(jnp.bfloat16)
    grad_pre_up = (grad_hidden * active).astype(jnp.bfloat16)
    grad_rows = jnp.dot(grad_pre_gate, gate_mat.T, preferred_element_type=jnp.float32)
    grad_rows = grad_rows + jnp.dot(grad_pre_up, up_mat.T, preferred_element_type=jnp.float32)
    weight_gate = jnp.dot(rows_x.T, grad_pre_gate, preferred_element_type=jnp.float32).astype(jnp.bfloat16)
    weight_up = jnp.dot(rows_x.T, grad_pre_up, preferred_element_type=jnp.float32).astype(jnp.bfloat16)
    weight_down = jnp.dot(rows_do.T, hidden, preferred_element_type=jnp.float32).astype(jnp.bfloat16)
    return expert_out, grad_rows, weight_gate, weight_up, weight_down


def reference(tokens, routes, scores, w_gate, w_up, w_down, cotangent):
    blocks_total = TOKENS // TOK_DEV
    pair_count = TOK_DEV * TOP
    gate_vals = route_scale * scores / jnp.sum(scores, axis=1, keepdims=True)
    block_routes = routes.reshape(blocks_total, pair_count)
    onehot = (block_routes[:, :, None] == jnp.arange(EXPERTS, dtype=jnp.int32)[None, None, :]).astype(jnp.int32)
    before = jnp.cumsum(onehot, axis=1) - onehot
    slot_rank = jnp.sum(before * onehot, axis=2).reshape(-1).astype(jnp.int32)
    expert_ids = block_routes.reshape(-1).astype(jnp.int32)
    pair_index = jnp.arange(TOKENS * TOP, dtype=jnp.int32)
    block_ids = (pair_index // pair_count).astype(jnp.int32)
    token_ids = (pair_index // TOP).astype(jnp.int32)
    gate_pairs = gate_vals.reshape(-1)
    x_slots = jnp.zeros((EXPERTS, blocks_total, CAP, D), tokens.dtype)
    x_slots = x_slots.at[expert_ids, block_ids, slot_rank].set(tokens[token_ids])
    do_pairs = (gate_pairs[:, None] * cotangent[token_ids].astype(jnp.float32)).astype(jnp.bfloat16)
    do_slots = jnp.zeros((EXPERTS, blocks_total, CAP, D), do_pairs.dtype)
    do_slots = do_slots.at[expert_ids, block_ids, slot_rank].set(do_pairs)

    def per_expert(expert_id):
        rows_x = x_slots[expert_id].reshape(blocks_total * CAP, D)
        rows_do = do_slots[expert_id].reshape(blocks_total * CAP, D)
        return expert_pass(rows_x, rows_do, w_gate[expert_id], w_up[expert_id], w_down[expert_id])

    outs_all, grads_all, weight_gate, weight_up, weight_down = lax.map(per_expert, jnp.arange(EXPERTS, dtype=jnp.int32))
    outs_all = outs_all.reshape(EXPERTS, blocks_total, CAP, D)
    grads_all = grads_all.reshape(EXPERTS, blocks_total, CAP, D)
    picked_out = outs_all[expert_ids, block_ids, slot_rank]
    picked_grad = grads_all[expert_ids, block_ids, slot_rank]
    layer_out = jnp.zeros((TOKENS, D), jnp.float32).at[token_ids].add(gate_pairs[:, None] * picked_out)
    grad_tokens = jnp.zeros((TOKENS, D), jnp.float32).at[token_ids].add(picked_grad)
    return (layer_out.astype(jnp.bfloat16), grad_tokens.astype(jnp.bfloat16), weight_gate, weight_up, weight_down)
```

```python
import jax
import jax.numpy as jnp
from jax import lax
from jax.sharding import PartitionSpec as P

HID = 1024
EXPERTS = 32
CAP = 8
BF16 = jnp.bfloat16
F32 = jnp.float32

route_scale = 2.5


def slot_weights(routes, scores):
    tok_count, top_count = routes.shape
    flat_routes = routes.reshape(-1)
    onehot = (flat_routes[:, None] == jnp.arange(EXPERTS, dtype=jnp.int32)[None, :]).astype(
        jnp.int32
    )
    before = jnp.cumsum(onehot, axis=0) - onehot
    slot_rank = jnp.sum(before * onehot, axis=1)
    slot_ids = flat_routes * CAP + slot_rank
    pick = (
        jnp.arange(EXPERTS * CAP, dtype=jnp.int32)[:, None] == slot_ids[None, :]
    ).reshape(EXPERTS * CAP, tok_count, top_count)
    gate_vals = route_scale * scores / jnp.sum(scores, axis=1, keepdims=True)
    select = jnp.sum(jnp.where(pick, 1.0, 0.0), axis=2)
    weighted = jnp.sum(jnp.where(pick, gate_vals[None], 0.0), axis=2)
    return select, weighted


def dp_groups():
    count = lax.axis_size("dp")
    inner = 4
    outer = count // inner
    inner_groups = [[o * inner + i for i in range(inner)] for o in range(outer)]
    outer_groups = [[o * inner + i for o in range(outer)] for i in range(inner)]
    return inner_groups, outer_groups


def spread(block, groups):
    size = len(groups[0])
    sent = jnp.broadcast_to(block[None], (size,) + block.shape)
    got = lax.all_to_all(
        sent, "dp", split_axis=0, concat_axis=0, axis_index_groups=groups, tiled=True
    )
    return got.reshape((-1,) + block.shape[1:])


def local(tokens, routes, scores, w_gate, w_up, w_down, cotangent):
    dp_count = lax.axis_size("dp")
    ex_count = lax.axis_size("expert")
    width = tokens.shape[1]
    slots = EXPERTS * CAP
    share = HID // dp_count
    cols = ex_count * CAP
    gate_w, up_w, down_w = w_gate[0], w_up[0], w_down[0]

    select, weighted = slot_weights(routes, scores)
    both = jnp.concatenate([tokens, cotangent], axis=1)
    picked = jnp.dot(select.astype(BF16), both, preferred_element_type=F32)
    slot_gate = jnp.sum(weighted, axis=1, keepdims=True)
    lane = lax.broadcasted_iota(jnp.int32, (1, 2 * width), 1)
    sent = (picked * jnp.where(lane < width, 1.0, slot_gate)).astype(BF16)
    rows = lax.all_to_all(
        sent.reshape(ex_count, CAP, 2 * width), "expert", split_axis=0, concat_axis=0, tiled=True
    ).reshape(cols, 2 * width)
    x_rows, do_rows = rows[:, :width], rows[:, width:]

    def part(w, r):
        return lax.dot_general(
            w, r, (((0,), (1,)), ((), ())), preferred_element_type=F32
        ).astype(BF16).reshape(dp_count, share, cols)

    parts = jnp.concatenate(
        [part(gate_w, x_rows), part(up_w, x_rows), part(down_w, do_rows)], axis=1
    )
    parts = lax.all_to_all(parts, "dp", split_axis=0, concat_axis=0, tiled=True)
    own = jnp.sum(parts.astype(F32), axis=0)
    pre_gate, pre_up, grad_hidden = own[:share], own[share : 2 * share], own[2 * share :]
    sigma = jax.nn.sigmoid(pre_gate)
    active = pre_gate * sigma
    block = jnp.concatenate(
        [
            active * pre_up,
            grad_hidden * pre_up * sigma * (1.0 + pre_gate * (1.0 - sigma)),
            grad_hidden * active,
        ],
        axis=0,
    ).astype(BF16)

    inner_groups, outer_groups = dp_groups()
    full = spread(spread(block, inner_groups), outer_groups).reshape(dp_count, 3, share, cols)
    hidden = full[:, 0].reshape(HID, cols)
    grad_gate_pre = full[:, 1].reshape(HID, cols)
    grad_up_pre = full[:, 2].reshape(HID, cols)

    def back(act, w):
        return lax.dot_general(act, w, (((0,), (1,)), ((), ())), preferred_element_type=F32)

    outs = jnp.concatenate(
        [back(hidden, down_w), back(grad_gate_pre, gate_w) + back(grad_up_pre, up_w)], axis=1
    ).astype(BF16)
    home = lax.all_to_all(
        outs.reshape(ex_count, CAP, 2 * width), "expert", split_axis=0, concat_axis=0, tiled=True
    ).reshape(slots, 2 * width).astype(F32)

    def weight_grad(r, act):
        return lax.dot_general(
            r, act, (((0,), (1,)), ((), ())), preferred_element_type=F32
        ).astype(BF16)[None]

    grad_gate = weight_grad(x_rows, grad_gate_pre)
    grad_up = weight_grad(x_rows, grad_up_pre)
    grad_down = weight_grad(do_rows, hidden)

    def combine(mix, vals):
        return lax.dot_general(
            mix, vals, (((0,), (0,)), ((), ())), precision=lax.Precision.HIGHEST
        ).astype(BF16)

    layer_out = combine(weighted, home[:, :width])
    grad_tokens = combine(select, home[:, width:])
    return layer_out, grad_tokens, grad_gate, grad_up, grad_down


def solution(mesh):
    rows = P("expert", "dp")
    table = P("expert", None)
    weight = P("expert", "dp", None)
    return jax.shard_map(
        local,
        mesh=mesh,
        in_specs=(rows, table, table, weight, weight, weight, rows),
        out_specs=(rows, rows, weight, weight, weight),
        check_vma=False,
    )
```

```python
import jax
import jax.numpy as jnp
from jax import lax
from jax.sharding import PartitionSpec as P

HID = 1024
EXPERTS = 32
CAP = 8
BF16 = jnp.bfloat16
F32 = jnp.float32

route_scale = 2.5


def slot_weights(routes, scores):
    tok_count, top_count = routes.shape
    flat_routes = routes.reshape(-1)
    onehot = (flat_routes[:, None] == jnp.arange(EXPERTS, dtype=jnp.int32)[None, :]).astype(
        jnp.int32
    )
    before = jnp.cumsum(onehot, axis=0) - onehot
    slot_rank = jnp.sum(before * onehot, axis=1)
    slot_ids = flat_routes * CAP + slot_rank
    pick = (
        jnp.arange(EXPERTS * CAP, dtype=jnp.int32)[:, None] == slot_ids[None, :]
    ).reshape(EXPERTS * CAP, tok_count, top_count)
    gate_vals = route_scale * scores / jnp.sum(scores, axis=1, keepdims=True)
    select = jnp.sum(jnp.where(pick, 1.0, 0.0), axis=2)
    weighted = jnp.sum(jnp.where(pick, gate_vals[None], 0.0), axis=2)
    return select, weighted


INNER = 4


def y_groups():
    outer = lax.axis_size("dp") // INNER
    return [[o * INNER + i for o in range(outer)] for i in range(INNER)]


def y_swap(blocks):
    return lax.all_to_all(
        blocks, "dp", split_axis=0, concat_axis=0, axis_index_groups=y_groups(), tiled=True
    )


def z_send(block, step):
    pairs = [
        (d, d // INNER * INNER + (d + step) % INNER) for d in range(lax.axis_size("dp"))
    ]
    return lax.ppermute(block, "dp", pairs)


def z_place():
    return lax.rem(lax.axis_index("dp"), INNER)


def z_reduce(blocks):
    place = z_place()
    got = [
        z_send(
            lax.dynamic_index_in_dim(blocks, lax.rem(place + step, INNER), 0, keepdims=False), step
        )
        for step in range(1, INNER)
    ]
    total = lax.dynamic_index_in_dim(blocks, place, 0, keepdims=False).astype(F32)
    for block in got:
        total = total + block.astype(F32)
    return total


def z_gather(block):
    place = z_place()
    full = jnp.zeros((INNER,) + block.shape, block.dtype)
    full = lax.dynamic_update_index_in_dim(full, block, place, 0)
    for step in range(1, INNER):
        full = lax.dynamic_update_index_in_dim(
            full, z_send(block, step), lax.rem(place + INNER - step, INNER), 0
        )
    return full


def y_reduce(blocks):
    return jnp.sum(y_swap(blocks).astype(F32), axis=0)


def y_gather(block):
    outer = lax.axis_size("dp") // INNER
    return y_swap(jnp.broadcast_to(block[None], (outer,) + block.shape))


def pointwise(own):
    pre_gate, pre_up, grad_hidden = own[0], own[1], own[2]
    sigma = jax.nn.sigmoid(pre_gate)
    active = pre_gate * sigma
    return jnp.stack(
        [
            active * pre_up,
            grad_hidden * pre_up * sigma * (1.0 + pre_gate * (1.0 - sigma)),
            grad_hidden * active,
        ]
    ).astype(BF16)


def local(tokens, routes, scores, w_gate, w_up, w_down, cotangent):
    dp_count = lax.axis_size("dp")
    ex_count = lax.axis_size("expert")
    width = tokens.shape[1]
    slots = EXPERTS * CAP
    cols = ex_count * CAP
    gate_w, up_w, down_w = w_gate[0], w_up[0], w_down[0]

    select, weighted = slot_weights(routes, scores)
    both = jnp.concatenate([tokens, cotangent], axis=1)
    picked = jnp.dot(select.astype(BF16), both, preferred_element_type=F32)
    slot_gate = jnp.sum(weighted, axis=1, keepdims=True)
    lane = lax.broadcasted_iota(jnp.int32, (1, 2 * width), 1)
    sent = (picked * jnp.where(lane < width, 1.0, slot_gate)).astype(BF16)
    rows = lax.all_to_all(
        sent.reshape(ex_count, CAP, 2 * width), "expert", split_axis=0, concat_axis=0, tiled=True
    ).reshape(cols, 2 * width)
    x_rows, do_rows = rows[:, :width], rows[:, width:]

    outer = dp_count // INNER
    half = HID // 2
    rows_each = half // dp_count

    def part(w, r):
        return lax.dot_general(
            w, r, (((0,), (1,)), ((), ())), preferred_element_type=F32
        ).astype(BF16)

    parts = [part(gate_w, x_rows), part(up_w, x_rows), part(down_w, do_rows)]
    a = jnp.stack([p[:half].reshape(outer, INNER, rows_each, cols) for p in parts], axis=2)
    b = jnp.stack([p[half:].reshape(INNER, outer, rows_each, cols) for p in parts], axis=2)
    a, b = y_reduce(a), z_reduce(b).astype(BF16)
    a, b = lax.optimization_barrier((a, b))
    a, b = pointwise(z_reduce(a)), pointwise(y_reduce(b))
    a, b = lax.optimization_barrier((a, b))
    a, b = z_gather(a), y_gather(b)
    a, b = lax.optimization_barrier((a, b))
    a, b = y_gather(a), z_gather(b)

    def whole(index):
        return jnp.concatenate(
            [a[:, :, index].reshape(half, cols), b[:, :, index].reshape(half, cols)], axis=0
        )

    hidden, grad_gate_pre, grad_up_pre = whole(0), whole(1), whole(2)

    def back(act, w):
        return lax.dot_general(act, w, (((0,), (1,)), ((), ())), preferred_element_type=F32)

    outs = jnp.concatenate(
        [back(hidden, down_w), back(grad_gate_pre, gate_w) + back(grad_up_pre, up_w)], axis=1
    ).astype(BF16)
    home = lax.all_to_all(
        outs.reshape(ex_count, CAP, 2 * width), "expert", split_axis=0, concat_axis=0, tiled=True
    ).reshape(slots, 2 * width).astype(F32)

    def weight_grad(r, act):
        return lax.dot_general(
            r, act, (((0,), (1,)), ((), ())), preferred_element_type=F32
        ).astype(BF16)[None]

    grad_gate = weight_grad(x_rows, grad_gate_pre)
    grad_up = weight_grad(x_rows, grad_up_pre)
    grad_down = weight_grad(do_rows, hidden)

    def combine(mix, vals):
        return lax.dot_general(
            mix, vals, (((0,), (0,)), ((), ())), precision=lax.Precision.HIGHEST
        ).astype(BF16)

    layer_out = combine(weighted, home[:, :width])
    grad_tokens = combine(select, home[:, width:])
    return layer_out, grad_tokens, grad_gate, grad_up, grad_down


def solution(mesh):
    rows = P("expert", "dp")
    table = P("expert", None)
    weight = P("expert", "dp", None)
    return jax.shard_map(
        local,
        mesh=mesh,
        in_specs=(rows, table, table, weight, weight, weight, rows),
        out_specs=(rows, rows, weight, weight, weight),
        check_vma=False,
    )
```

```python
import jax
import jax.numpy as jnp
from jax import lax
from jax.sharding import PartitionSpec as P

HID = 1024
EXPERTS = 32
CAP = 8
BF16 = jnp.bfloat16
F32 = jnp.float32

route_scale = 2.5


def slot_weights(routes, scores):
    tok_count, top_count = routes.shape
    flat_routes = routes.reshape(-1)
    onehot = (flat_routes[:, None] == jnp.arange(EXPERTS, dtype=jnp.int32)[None, :]).astype(
        jnp.int32
    )
    before = jnp.cumsum(onehot, axis=0) - onehot
    slot_rank = jnp.sum(before * onehot, axis=1)
    slot_ids = flat_routes * CAP + slot_rank
    pick = (
        jnp.arange(EXPERTS * CAP, dtype=jnp.int32)[:, None] == slot_ids[None, :]
    ).reshape(EXPERTS * CAP, tok_count, top_count)
    gate_vals = route_scale * scores / jnp.sum(scores, axis=1, keepdims=True)
    select = jnp.sum(jnp.where(pick, 1.0, 0.0), axis=2)
    weighted = jnp.sum(jnp.where(pick, gate_vals[None], 0.0), axis=2)
    return select, weighted


INNER = 4


def parity_groups():
    pairs = lax.axis_size("dp") // INNER // 2
    return [
        [(2 * j + p) * INNER + z for j in range(pairs) for z in range(INNER)] for p in range(2)
    ]


def group_swap(blocks):
    return lax.all_to_all(
        blocks, "dp", split_axis=0, concat_axis=0, axis_index_groups=parity_groups(), tiled=True
    )


def neighbour_swap(block, side):
    count = lax.axis_size("dp")
    ring = count // INNER

    def other(y):
        return y ^ 1 if side == 0 else (y + 1 if y % 2 else y - 1) % ring

    pairs = [(d, other(d // INNER) * INNER + d % INNER) for d in range(count)]
    return lax.ppermute(block, "dp", pairs)


def local(tokens, routes, scores, w_gate, w_up, w_down, cotangent):
    dp_count = lax.axis_size("dp")
    ex_count = lax.axis_size("expert")
    width = tokens.shape[1]
    slots = EXPERTS * CAP
    cols = ex_count * CAP
    gate_w, up_w, down_w = w_gate[0], w_up[0], w_down[0]

    select, weighted = slot_weights(routes, scores)
    both = jnp.concatenate([tokens, cotangent], axis=1)
    picked = jnp.dot(select.astype(BF16), both, preferred_element_type=F32)
    slot_gate = jnp.sum(weighted, axis=1, keepdims=True)
    lane = lax.broadcasted_iota(jnp.int32, (1, 2 * width), 1)
    sent = (picked * jnp.where(lane < width, 1.0, slot_gate)).astype(BF16)
    rows = lax.all_to_all(
        sent.reshape(ex_count, CAP, 2 * width), "expert", split_axis=0, concat_axis=0, tiled=True
    ).reshape(cols, 2 * width)
    x_rows, do_rows = rows[:, :width], rows[:, width:]

    group = dp_count // 2
    rows_each = HID // dp_count // 2
    odd = lax.rem(lax.axis_index("dp") // INNER, 2) == 1

    def part(w, r):
        return lax.dot_general(
            w, r, (((0,), (1,)), ((), ())), preferred_element_type=F32
        ).reshape(2, 2, group, rows_each, cols)

    parts = [part(gate_w, x_rows), part(up_w, x_rows), part(down_w, do_rows)]

    def summed(side):
        mine = jnp.stack([jnp.where(odd, p[1, side], p[0, side]) for p in parts], axis=1)
        sent = jnp.stack([jnp.where(odd, p[0, side], p[1, side]) for p in parts], axis=1)
        return (mine + neighbour_swap(sent.astype(BF16), side).astype(F32)).astype(BF16)

    pair_sums = jnp.stack([summed(0), summed(1)], axis=1)
    own = jnp.sum(group_swap(pair_sums).astype(F32), axis=0)
    pre_gate, pre_up, grad_hidden = own[:, 0], own[:, 1], own[:, 2]
    sigma = jax.nn.sigmoid(pre_gate)
    active = pre_gate * sigma
    block = jnp.stack(
        [
            active * pre_up,
            grad_hidden * pre_up * sigma * (1.0 + pre_gate * (1.0 - sigma)),
            grad_hidden * active,
        ],
        axis=1,
    ).astype(BF16)
    near = group_swap(jnp.broadcast_to(block[None], (group,) + block.shape))
    near = [near[:, 0], near[:, 1]]
    far = [neighbour_swap(near[0], 0), neighbour_swap(near[1], 1)]

    def whole(index):
        own_rows = jnp.stack([near[0][:, index], near[1][:, index]])
        far_rows = jnp.stack([far[0][:, index], far[1][:, index]])
        return jnp.stack(
            [jnp.where(odd, far_rows, own_rows), jnp.where(odd, own_rows, far_rows)]
        ).reshape(HID, cols)

    hidden, grad_gate_pre, grad_up_pre = whole(0), whole(1), whole(2)

    def back(act, w):
        return lax.dot_general(act, w, (((0,), (1,)), ((), ())), preferred_element_type=F32)

    outs = jnp.concatenate(
        [back(hidden, down_w), back(grad_gate_pre, gate_w) + back(grad_up_pre, up_w)], axis=1
    ).astype(BF16)
    home = lax.all_to_all(
        outs.reshape(ex_count, CAP, 2 * width), "expert", split_axis=0, concat_axis=0, tiled=True
    ).reshape(slots, 2 * width).astype(F32)

    def weight_grad(r, act):
        return lax.dot_general(
            r, act, (((0,), (1,)), ((), ())), preferred_element_type=F32
        ).astype(BF16)[None]

    grad_gate = weight_grad(x_rows, grad_gate_pre)
    grad_up = weight_grad(x_rows, grad_up_pre)
    grad_down = weight_grad(do_rows, hidden)

    def combine(mix, vals):
        return lax.dot_general(
            mix, vals, (((0,), (0,)), ((), ())), precision=lax.Precision.HIGHEST
        ).astype(BF16)

    layer_out = combine(weighted, home[:, :width])
    grad_tokens = combine(select, home[:, width:])
    return layer_out, grad_tokens, grad_gate, grad_up, grad_down


def solution(mesh):
    rows = P("expert", "dp")
    table = P("expert", None)
    weight = P("expert", "dp", None)
    return jax.shard_map(
        local,
        mesh=mesh,
        in_specs=(rows, table, table, weight, weight, weight, rows),
        out_specs=(rows, rows, weight, weight, weight),
        check_vma=False,
    )
```

```python
import jax
import jax.numpy as jnp
from jax import lax
from jax.experimental import pallas as pl
from jax.experimental.pallas import tpu as pltpu
from jax.sharding import PartitionSpec as P

HID = 1024
EXPERTS = 32
CAP = 8
BF16 = jnp.bfloat16
F32 = jnp.float32
INNER = 4
LANES = 128

route_scale = 2.5


def pitch_of(width):
    return -(-width // LANES) * LANES


def flip(block):
    return block.astype(F32).T.astype(BF16)


def pick_kernel(routes_ref, scores_ref, tokens_ref, cotangent_ref, sent_ref, mix_ref, pick_ref):
    tok_count, top_count = routes_ref.shape
    slots = sent_ref.shape[0]
    width = tokens_ref.shape[1]
    pitch = sent_ref.shape[1] // 2
    scores = scores_ref[...]
    gates = route_scale * scores / jnp.sum(scores, axis=1, keepdims=True)
    routes = routes_ref[...]
    slot = lax.broadcasted_iota(jnp.int32, (tok_count, slots), 1)
    shift = CAP.bit_length() - 1
    expert, rank = slot >> shift, slot & (CAP - 1)
    hit = jnp.zeros((tok_count, slots), F32)
    gate = jnp.zeros((tok_count, slots), F32)
    for k in range(top_count):
        same = routes[:, k : k + 1] == expert
        hit = hit + jnp.where(same, 1.0, 0.0)
        gate = gate + jnp.where(same, gates[:, k : k + 1], 0.0)
    row = lax.broadcasted_iota(jnp.int32, (tok_count, tok_count), 0)
    col = lax.broadcasted_iota(jnp.int32, (tok_count, tok_count), 1)
    earlier = jnp.where(col < row, 1.0, 0.0).astype(BF16)
    before = jnp.dot(earlier, hit.astype(BF16), preferred_element_type=F32)
    pick = jnp.where(before == rank.astype(F32), hit, 0.0)
    mix = pick * gate
    mix_ref[...] = mix
    pick_ref[...] = pick.astype(BF16)
    picker = pick.T.astype(BF16)
    slot_gate = jnp.sum(mix.T, axis=1, keepdims=True)
    sent_ref[...] = jnp.zeros(sent_ref.shape, BF16)
    rows = jnp.dot(picker, tokens_ref[...], preferred_element_type=F32)
    sent_ref[:, :width] = rows.astype(BF16)
    rows = jnp.dot(picker, cotangent_ref[...], preferred_element_type=F32)
    sent_ref[:, pitch : pitch + width] = (rows * slot_gate).astype(BF16)


def start_of(odd, other, side, span):
    parity = 1 - odd if other else odd
    return pl.multiple_of((parity * 2 + side) * span, span)


def part_kernel(odd_ref, rows_ref, gate_ref, up_ref, down_ref, own_ref, sent_ref):
    odd = odd_ref[0]
    width = gate_ref.shape[0]
    pitch = rows_ref.shape[1] // 2
    _, group, depth, cols = own_ref.shape
    each = depth // 3
    span = group * each
    x = flip(rows_ref[:, :width])
    do = flip(rows_ref[:, pitch : pitch + width])
    for side in range(2):
        for other, to_ref in ((True, sent_ref), (False, own_ref)):
            start = start_of(odd, other, side, span)
            for index, (w_ref, r) in enumerate(((gate_ref, x), (up_ref, x), (down_ref, do))):
                part = lax.dot_general(
                    w_ref[:, pl.ds(start, span)],
                    r,
                    (((0,), (0,)), ((), ())),
                    preferred_element_type=F32,
                )
                to_ref[side, :, index * each : (index + 1) * each, :] = part.reshape(
                    group, each, cols
                ).astype(to_ref.dtype)


def pieces(odd, near_ref, far_refs):
    group, _, depth, cols = near_ref.shape
    each = depth // 3
    span = group * each
    for side in range(2):
        for other in (False, True):
            source = far_refs[side] if other else near_ref.at[:, side]
            blocks = [
                source[:, index * each : (index + 1) * each, :].reshape(span, cols)
                for index in range(3)
            ]
            yield start_of(odd, other, side, span), span, blocks


def out_kernel(odd_ref, near_ref, far0_ref, far1_ref, gate_ref, up_ref, down_ref, outs_ref):
    width = gate_ref.shape[0]
    pitch = outs_ref.shape[1] // 2
    cols = outs_ref.shape[0]
    out = jnp.zeros((width, cols), F32)
    grad = jnp.zeros((width, cols), F32)
    for start, span, blocks in pieces(odd_ref[0], near_ref, (far0_ref, far1_ref)):
        hidden, grad_gate, grad_up = blocks

        def times(w_ref, block):
            return jnp.dot(w_ref[:, pl.ds(start, span)], block, preferred_element_type=F32)

        out = out + times(down_ref, hidden)
        grad = grad + times(gate_ref, grad_gate) + times(up_ref, grad_up)
    outs_ref[...] = jnp.zeros(outs_ref.shape, BF16)
    outs_ref[:, :width] = out.T.astype(BF16)
    outs_ref[:, pitch : pitch + width] = grad.T.astype(BF16)


def grad_kernel(odd_ref, near_ref, far0_ref, far1_ref, rows_ref, gate_ref, up_ref, down_ref):
    width = gate_ref.shape[0]
    pitch = rows_ref.shape[1] // 2
    x = flip(rows_ref[:, :width])
    do = flip(rows_ref[:, pitch : pitch + width])
    for start, span, blocks in pieces(odd_ref[0], near_ref, (far0_ref, far1_ref)):
        hidden, grad_gate, grad_up = blocks
        for to_ref, r, block in ((gate_ref, x, grad_gate), (up_ref, x, grad_up), (down_ref, do, hidden)):
            to_ref[:, pl.ds(start, span)] = lax.dot_general(
                r, block, (((1,), (1,)), ((), ())), preferred_element_type=F32
            ).astype(BF16)


def combine_kernel(home_ref, mix_ref, pick_ref, out_ref, grad_ref):
    width = out_ref.shape[1]
    pitch = home_ref.shape[1] // 2
    out_ref[...] = jnp.dot(
        mix_ref[...],
        home_ref[:, :width].astype(F32),
        precision=lax.Precision.HIGHEST,
        preferred_element_type=F32,
    ).astype(BF16)
    grad_ref[...] = jnp.dot(
        pick_ref[...], home_ref[:, pitch : pitch + width], preferred_element_type=F32
    ).astype(BF16)


VMEM = pl.BlockSpec(memory_space=pltpu.VMEM)
SMEM = pl.BlockSpec(memory_space=pltpu.SMEM)


def run(kernel, outs, args, flops):
    outs = [jax.ShapeDtypeStruct(shape, dtype) for shape, dtype in outs]
    moved = sum(a.size * a.dtype.itemsize for a in list(args) + outs)
    return pl.pallas_call(
        kernel,
        out_shape=outs,
        in_specs=[SMEM if a.shape == (1,) else VMEM for a in args],
        out_specs=[VMEM] * len(outs),
        cost_estimate=pl.CostEstimate(flops=flops, bytes_accessed=moved, transcendentals=0),
    )(*args)


def parity_groups():
    pairs = lax.axis_size("dp") // INNER // 2
    return [
        [(2 * j + p) * INNER + z for j in range(pairs) for z in range(INNER)] for p in range(2)
    ]


def group_swap(blocks):
    return lax.all_to_all(
        blocks, "dp", split_axis=0, concat_axis=0, axis_index_groups=parity_groups(), tiled=True
    )


def neighbour_swap(block, side):
    count = lax.axis_size("dp")
    ring = count // INNER

    def other(y):
        return y ^ 1 if side == 0 else (y + 1 if y % 2 else y - 1) % ring

    pairs = [(d, other(d // INNER) * INNER + d % INNER) for d in range(count)]
    return lax.ppermute(block, "dp", pairs)


def expert_swap(rows):
    count = lax.axis_size("expert")
    got = lax.all_to_all(
        rows.reshape(count, CAP, rows.shape[1]),
        "expert",
        split_axis=0,
        concat_axis=0,
        tiled=True,
    )
    return got.reshape(rows.shape)


def local(tokens, routes, scores, w_gate, w_up, w_down, cotangent):
    tok_count, width = tokens.shape
    slots = EXPERTS * CAP
    pitch = pitch_of(width)
    group = lax.axis_size("dp") // 2
    each = HID // lax.axis_size("dp") // 2
    depth = 3 * each
    weights = (w_gate[0], w_up[0], w_down[0])
    odd = lax.rem(lax.axis_index("dp") // INNER, 2).astype(jnp.int32).reshape(1)
    work = 6 * slots * HID * width

    sent, mix, pick = run(
        pick_kernel,
        [((slots, 2 * pitch), BF16), ((tok_count, slots), F32), ((tok_count, slots), BF16)],
        (routes, scores, tokens, cotangent),
        4 * slots * tok_count * width,
    )
    rows = expert_swap(sent)
    cols = rows.shape[0]
    shape = (2, group, depth, cols)
    own, sent = run(part_kernel, [(shape, F32), (shape, BF16)], (odd, rows) + weights, work)
    pair_sums = jnp.stack(
        [(own[s] + neighbour_swap(sent[s], s).astype(F32)).astype(BF16) for s in range(2)], axis=1
    )
    own = jnp.sum(group_swap(pair_sums).astype(F32), axis=0)
    pre_gate, pre_up, grad_hidden = own[:, :each], own[:, each : 2 * each], own[:, 2 * each :]
    sigma = jax.nn.sigmoid(pre_gate)
    active = pre_gate * sigma
    block = jnp.concatenate(
        [
            active * pre_up,
            grad_hidden * pre_up * sigma * (1.0 + pre_gate * (1.0 - sigma)),
            grad_hidden * active,
        ],
        axis=1,
    ).astype(BF16)
    near = group_swap(jnp.broadcast_to(block[None], (group,) + block.shape))
    full = (odd, near, neighbour_swap(near[:, 0], 0), neighbour_swap(near[:, 1], 1))
    (outs,) = run(out_kernel, [((cols, 2 * pitch), BF16)], full + weights, work)
    home = expert_swap(outs)
    grads = run(grad_kernel, [((width, HID), BF16)] * 3, full + (rows,), work)
    layer_out, grad_tokens = run(
        combine_kernel,
        [((tok_count, width), BF16)] * 2,
        (home, mix, pick),
        4 * slots * tok_count * width,
    )
    return (layer_out, grad_tokens) + tuple(g[None] for g in grads)


def solution(mesh):
    rows = P("expert", "dp")
    table = P("expert", None)
    weight = P("expert", "dp", None)
    return jax.shard_map(
        local,
        mesh=mesh,
        in_specs=(rows, table, table, weight, weight, weight, rows),
        out_specs=(rows, rows, weight, weight, weight),
        check_vma=False,
    )
```

```python
import jax
import jax.numpy as jnp
from jax import lax
from jax.experimental import pallas as pl
from jax.experimental.pallas import tpu as pltpu
from jax.sharding import PartitionSpec as P

HID = 1024
EXPERTS = 32
CAP = 8
BF16 = jnp.bfloat16
F32 = jnp.float32
INNER = 4
LANES = 128

route_scale = 2.5


def pitch_of(width):
    return -(-width // LANES) * LANES


def flip(block):
    return block.astype(F32).T.astype(BF16)


def pick_kernel(routes_ref, scores_ref, tokens_ref, cotangent_ref, sent_ref, mix_ref):
    top_count, tok_count = routes_ref.shape
    slots = sent_ref.shape[0]
    width = tokens_ref.shape[1]
    pitch = sent_ref.shape[1] // 2
    scores = scores_ref[...].T
    gates = route_scale * scores / jnp.sum(scores, axis=1, keepdims=True)
    routes = routes_ref[...].astype(F32).T.astype(jnp.int32)
    slot = lax.broadcasted_iota(jnp.int32, (tok_count, slots), 1)
    shift = CAP.bit_length() - 1
    expert, rank = slot >> shift, slot & (CAP - 1)
    hit = jnp.zeros((tok_count, slots), F32)
    gate = jnp.zeros((tok_count, slots), F32)
    for k in range(top_count):
        same = routes[:, k : k + 1] == expert
        hit = hit + jnp.where(same, 1.0, 0.0)
        gate = gate + jnp.where(same, gates[:, k : k + 1], 0.0)
    row = lax.broadcasted_iota(jnp.int32, (tok_count, tok_count), 0)
    col = lax.broadcasted_iota(jnp.int32, (tok_count, tok_count), 1)
    earlier = jnp.where(col < row, 1.0, 0.0).astype(BF16)
    before = jnp.dot(earlier, hit.astype(BF16), preferred_element_type=F32)
    pick = jnp.where(before == rank.astype(F32), hit, 0.0)
    mix = pick * gate
    high = mix.astype(BF16)
    rest = mix - high.astype(F32)
    middle = rest.astype(BF16)
    low = (rest - middle.astype(F32)).astype(BF16)
    for index, term in enumerate((pick.astype(BF16), high, middle, low)):
        mix_ref[index * tok_count : (index + 1) * tok_count, :] = term
    picker = pick.T.astype(BF16)
    slot_gate = jnp.sum(mix.T, axis=1, keepdims=True)
    sent_ref[...] = jnp.zeros(sent_ref.shape, BF16)
    rows = jnp.dot(picker, tokens_ref[...], preferred_element_type=F32)
    sent_ref[:, :width] = rows.astype(BF16)
    rows = jnp.dot(picker, cotangent_ref[...], preferred_element_type=F32)
    sent_ref[:, pitch : pitch + width] = (rows * slot_gate).astype(BF16)


def start_of(odd, other, side, span):
    parity = 1 - odd if other else odd
    return pl.multiple_of((parity * 2 + side) * span, span)


def part_kernel(other, sides):
    def kernel(odd_ref, rows_ref, gate_ref, up_ref, down_ref, *to_refs):
        width = gate_ref.shape[0]
        pitch = rows_ref.shape[1] // 2
        group, depth, cols = to_refs[0].shape
        each = depth // 3
        span = group * each
        x = flip(rows_ref[:, :width])
        do = flip(rows_ref[:, pitch : pitch + width])
        for side, to_ref in zip(sides, to_refs):
            start = start_of(odd_ref[0], other, side, span)
            for index, (w_ref, r) in enumerate(((gate_ref, x), (up_ref, x), (down_ref, do))):
                part = lax.dot_general(
                    w_ref[:, pl.ds(start, span)],
                    r,
                    (((0,), (0,)), ((), ())),
                    preferred_element_type=F32,
                )
                to_ref[:, index * each : (index + 1) * each, :] = part.reshape(
                    group, each, cols
                ).astype(to_ref.dtype)

    return kernel


def pieces(odd, near_ref, far_refs, others):
    sample = far_refs[0] if near_ref is None else near_ref
    group, depth, cols = sample.shape[0], sample.shape[-2], sample.shape[-1]
    each = depth // 3
    span = group * each
    for side in range(2):
        for other in others:
            source = far_refs[side] if other else near_ref.at[:, side]
            blocks = [
                source[:, index * each : (index + 1) * each, :].reshape(span, cols)
                for index in range(3)
            ]
            yield start_of(odd, other, side, span), span, blocks


def out_terms(parts, gate_ref, up_ref, down_ref, out, grad):
    for start, span, blocks in parts:
        hidden, grad_gate, grad_up = blocks

        def times(w_ref, block):
            return jnp.dot(w_ref[:, pl.ds(start, span)], block, preferred_element_type=F32)

        out = out + times(down_ref, hidden)
        grad = grad + times(gate_ref, grad_gate) + times(up_ref, grad_up)
    return out, grad


def near_kernel(odd_ref, near_ref, gate_ref, up_ref, down_ref, out_ref, grad_ref):
    zero = jnp.zeros(out_ref.shape, F32)
    parts = pieces(odd_ref[0], near_ref, None, (False,))
    out_ref[...], grad_ref[...] = out_terms(parts, gate_ref, up_ref, down_ref, zero, zero)


def far_kernel(
    odd_ref, far0_ref, far1_ref, gate_ref, up_ref, down_ref, out_ref, grad_ref, outs_ref
):
    width = gate_ref.shape[0]
    pitch = outs_ref.shape[1] // 2
    parts = pieces(odd_ref[0], None, (far0_ref, far1_ref), (True,))
    out, grad = out_terms(parts, gate_ref, up_ref, down_ref, out_ref[...], grad_ref[...])
    outs_ref[...] = jnp.zeros(outs_ref.shape, BF16)
    outs_ref[:, :width] = out.T.astype(BF16)
    outs_ref[:, pitch : pitch + width] = grad.T.astype(BF16)


def grad_kernel(odd_ref, near_ref, far0_ref, far1_ref, rows_ref, gate_ref, up_ref, down_ref):
    width = gate_ref.shape[0]
    pitch = rows_ref.shape[1] // 2
    x = flip(rows_ref[:, :width])
    do = flip(rows_ref[:, pitch : pitch + width])
    for start, span, blocks in pieces(
        odd_ref[0], near_ref, (far0_ref, far1_ref), (False, True)
    ):
        hidden, grad_gate, grad_up = blocks
        for to_ref, r, block in ((gate_ref, x, grad_gate), (up_ref, x, grad_up), (down_ref, do, hidden)):
            to_ref[:, pl.ds(start, span)] = lax.dot_general(
                r, block, (((1,), (1,)), ((), ())), preferred_element_type=F32
            ).astype(BF16)


def combine_kernel(home_ref, mix_ref, out_ref, grad_ref):
    rows, width = out_ref.shape
    pitch = home_ref.shape[1] // 2
    sums = jnp.dot(mix_ref[...], home_ref[...], preferred_element_type=F32)
    gated = sums[rows : 2 * rows] + sums[2 * rows : 3 * rows] + sums[3 * rows :]
    out_ref[...] = gated[:, :width].astype(BF16)
    grad_ref[...] = sums[:rows, pitch : pitch + width].astype(BF16)


VMEM = pl.BlockSpec(memory_space=pltpu.VMEM)
SMEM = pl.BlockSpec(memory_space=pltpu.SMEM)


def run(kernel, outs, args, flops, grant=16):
    outs = [jax.ShapeDtypeStruct(shape, dtype) for shape, dtype in outs]
    moved = sum(a.size * a.dtype.itemsize for a in list(args) + outs)
    return pl.pallas_call(
        kernel,
        out_shape=outs,
        in_specs=[SMEM if a.shape == (1,) else VMEM for a in args],
        out_specs=[VMEM] * len(outs),
        compiler_params=pltpu.CompilerParams(vmem_limit_bytes=grant * 2**20),
        cost_estimate=pl.CostEstimate(flops=flops, bytes_accessed=moved, transcendentals=0),
    )(*args)


def parity_groups():
    pairs = lax.axis_size("dp") // INNER // 2
    return [
        [(2 * j + p) * INNER + z for j in range(pairs) for z in range(INNER)] for p in range(2)
    ]


def group_swap(blocks):
    return lax.all_to_all(
        blocks, "dp", split_axis=0, concat_axis=0, axis_index_groups=parity_groups(), tiled=True
    )


def neighbour_swap(block, side):
    count = lax.axis_size("dp")
    ring = count // INNER

    def other(y):
        return y ^ 1 if side == 0 else (y + 1 if y % 2 else y - 1) % ring

    pairs = [(d, other(d // INNER) * INNER + d % INNER) for d in range(count)]
    return lax.ppermute(block, "dp", pairs)


def expert_swap(rows):
    count = lax.axis_size("expert")
    got = lax.all_to_all(
        rows.reshape(count, CAP, rows.shape[1]),
        "expert",
        split_axis=0,
        concat_axis=0,
        tiled=True,
    )
    return got.reshape(rows.shape)


def local(tokens, routes, scores, w_gate, w_up, w_down, cotangent):
    tok_count, width = tokens.shape
    slots = EXPERTS * CAP
    pitch = pitch_of(width)
    group = lax.axis_size("dp") // 2
    each = HID // lax.axis_size("dp") // 2
    depth = 3 * each
    weights = (w_gate[0], w_up[0], w_down[0])
    odd = lax.rem(lax.axis_index("dp") // INNER, 2).astype(jnp.int32).reshape(1)
    work = 6 * slots * HID * width

    sent, mix = run(
        pick_kernel,
        [((slots, 2 * pitch), BF16), ((4 * tok_count, slots), BF16)],
        (routes.T, scores.T, tokens, cotangent),
        4 * slots * tok_count * width,
    )
    rows = expert_swap(sent)
    cols = rows.shape[0]
    shape = (group, depth, cols)
    inputs = (odd, rows) + weights
    got = []
    for side in range(2):
        (sent,) = run(part_kernel(True, (side,)), [(shape, BF16)], inputs, work // 4)
        got.append(neighbour_swap(sent, side))
    own = run(part_kernel(False, (0, 1)), [(shape, F32)] * 2, inputs, work // 2)
    pair_sums = jnp.stack([(o + g.astype(F32)).astype(BF16) for o, g in zip(own, got)], axis=1)
    own = jnp.sum(group_swap(pair_sums).astype(F32), axis=0)
    pre_gate, pre_up, grad_hidden = own[:, :each], own[:, each : 2 * each], own[:, 2 * each :]
    sigma = jax.nn.sigmoid(pre_gate)
    active = pre_gate * sigma
    block = jnp.concatenate(
        [
            active * pre_up,
            grad_hidden * pre_up * sigma * (1.0 + pre_gate * (1.0 - sigma)),
            grad_hidden * active,
        ],
        axis=1,
    ).astype(BF16)
    near = group_swap(jnp.broadcast_to(block[None], (group,) + block.shape))
    far = tuple(neighbour_swap(near[:, side], side) for side in range(2))
    halves = run(near_kernel, [((width, cols), F32)] * 2, (odd, near) + weights, work // 2)
    (outs,) = run(
        far_kernel, [((cols, 2 * pitch), BF16)], (odd,) + far + weights + tuple(halves), work // 2
    )
    home = expert_swap(outs)
    grads = run(grad_kernel, [((width, HID), BF16)] * 3, (odd, near) + far + (rows,), work)
    layer_out, grad_tokens = run(
        combine_kernel,
        [((tok_count, width), BF16)] * 2,
        (home, mix),
        16 * slots * tok_count * width,
    )
    return (layer_out, grad_tokens) + tuple(g[None] for g in grads)


def solution(mesh):
    rows = P("expert", "dp")
    table = P("expert", None)
    weight = P("expert", "dp", None)
    return jax.shard_map(
        local,
        mesh=mesh,
        in_specs=(rows, table, table, weight, weight, weight, rows),
        out_specs=(rows, rows, weight, weight, weight),
        check_vma=False,
    )
```

```python
import jax
import jax.numpy as jnp
from jax import lax
from jax.experimental import pallas as pl
from jax.experimental.pallas import tpu as pltpu
from jax.sharding import PartitionSpec as P

HID = 1024
EXPERTS = 32
CAP = 8
BF16 = jnp.bfloat16
F32 = jnp.float32
INNER = 4
LANES = 128

route_scale = 2.5


def pitch_of(width):
    return -(-width // LANES) * LANES


def flip(block):
    return block.astype(F32).T.astype(BF16)


def pick_kernel(routes_ref, scores_ref, tokens_ref, cotangent_ref, sent_ref, mix_ref):
    top_count, tok_count = routes_ref.shape
    slots = sent_ref.shape[0]
    width = tokens_ref.shape[1]
    pitch = sent_ref.shape[1] // 2
    scores = scores_ref[...].T
    gates = route_scale * scores / jnp.sum(scores, axis=1, keepdims=True)
    routes = routes_ref[...].astype(F32).T.astype(jnp.int32)
    slot = lax.broadcasted_iota(jnp.int32, (tok_count, slots), 1)
    shift = CAP.bit_length() - 1
    expert, rank = slot >> shift, slot & (CAP - 1)
    hit = jnp.zeros((tok_count, slots), F32)
    gate = jnp.zeros((tok_count, slots), F32)
    for k in range(top_count):
        same = routes[:, k : k + 1] == expert
        hit = hit + jnp.where(same, 1.0, 0.0)
        gate = gate + jnp.where(same, gates[:, k : k + 1], 0.0)
    row = lax.broadcasted_iota(jnp.int32, (tok_count, tok_count), 0)
    col = lax.broadcasted_iota(jnp.int32, (tok_count, tok_count), 1)
    earlier = jnp.where(col < row, 1.0, 0.0).astype(BF16)
    before = jnp.dot(earlier, hit.astype(BF16), preferred_element_type=F32)
    pick = jnp.where(before == rank.astype(F32), hit, 0.0)
    mix = pick * gate
    high = mix.astype(BF16)
    rest = mix - high.astype(F32)
    middle = rest.astype(BF16)
    low = (rest - middle.astype(F32)).astype(BF16)
    for index, term in enumerate((pick.astype(BF16), high, middle, low)):
        mix_ref[index * tok_count : (index + 1) * tok_count, :] = term
    picker = pick.T.astype(BF16)
    slot_gate = jnp.sum(mix.T, axis=1, keepdims=True)
    sent_ref[...] = jnp.zeros(sent_ref.shape, BF16)
    rows = jnp.dot(picker, tokens_ref[...], preferred_element_type=F32)
    sent_ref[:, :width] = rows.astype(BF16)
    rows = jnp.dot(picker, cotangent_ref[...], preferred_element_type=F32)
    sent_ref[:, pitch : pitch + width] = (rows * slot_gate).astype(BF16)


def row_kernel(base):
    def kernel(rows_ref, gate_ref, up_ref, down_ref, *refs):
        to_ref = refs[-1]
        width, span = gate_ref.shape
        pitch = rows_ref.shape[1] // 2
        group, depth, cols = to_ref.shape
        each = depth // 3
        x = flip(rows_ref[:, :width])
        do = flip(rows_ref[:, pitch : pitch + width])
        for index, (w_ref, r) in enumerate(((gate_ref, x), (up_ref, x), (down_ref, do))):
            part = lax.dot_general(
                w_ref[...], r, (((0,), (0,)), ((), ())), preferred_element_type=F32
            ).reshape(group, each, cols)
            at = pl.ds(index * each, each)
            if base:
                part = part + refs[0][:, at, :]
            to_ref[:, at, :] = part.astype(to_ref.dtype)

    return kernel


def array_rows(ref, index):
    group, depth, cols = ref.shape
    each = depth // 3
    return ref[:, index * each : (index + 1) * each, :].reshape(group * each, cols)


def out_kernel(near_ref, gate_ref, up_ref, down_ref, outs_ref):
    width = gate_ref.shape[0]
    pitch = outs_ref.shape[1] // 2

    def times(w_ref, index):
        return jnp.dot(w_ref[...], array_rows(near_ref, index), preferred_element_type=F32)

    out = times(down_ref, 0)
    grad = times(gate_ref, 1) + times(up_ref, 2)
    outs_ref[...] = jnp.zeros(outs_ref.shape, outs_ref.dtype)
    outs_ref[:, :width] = out.T.astype(outs_ref.dtype)
    outs_ref[:, pitch : pitch + width] = grad.T.astype(outs_ref.dtype)


def grad_kernel(odd_ref, near_ref, far0_ref, far1_ref, rows_ref, gate_ref, up_ref, down_ref):
    odd = odd_ref[0]
    width = gate_ref.shape[0]
    pitch = rows_ref.shape[1] // 2
    half = gate_ref.shape[1] // 2
    x = flip(rows_ref[:, :width])
    do = flip(rows_ref[:, pitch : pitch + width])
    places = ((near_ref, odd * half), (far0_ref, (1 - odd) * half))
    places += ((far1_ref, (1 - odd) * half + half // 2),)
    for ref, start in places:
        for to_ref, r, index in ((gate_ref, x, 1), (up_ref, x, 2), (down_ref, do, 0)):
            block = array_rows(ref, index)
            span = block.shape[0]
            to_ref[:, pl.ds(pl.multiple_of(start, half // 2), span)] = lax.dot_general(
                r, block, (((1,), (1,)), ((), ())), preferred_element_type=F32
            ).astype(BF16)


def combine_kernel(home_ref, mix_ref, out_ref, grad_ref):
    rows, width = out_ref.shape
    pitch = home_ref.shape[1] // 2
    sums = jnp.dot(mix_ref[...], home_ref[...], preferred_element_type=F32)
    gated = sums[rows : 2 * rows] + sums[2 * rows : 3 * rows] + sums[3 * rows :]
    out_ref[...] = gated[:, :width].astype(BF16)
    grad_ref[...] = sums[:rows, pitch : pitch + width].astype(BF16)


VMEM = pl.BlockSpec(memory_space=pltpu.VMEM)
SMEM = pl.BlockSpec(memory_space=pltpu.SMEM)


def run(kernel, outs, args, flops, grant=16):
    outs = [jax.ShapeDtypeStruct(shape, dtype) for shape, dtype in outs]
    moved = sum(a.size * a.dtype.itemsize for a in list(args) + outs)
    return pl.pallas_call(
        kernel,
        out_shape=outs,
        in_specs=[SMEM if a.shape == (1,) else VMEM for a in args],
        out_specs=[VMEM] * len(outs),
        compiler_params=pltpu.CompilerParams(vmem_limit_bytes=grant and grant * 2**20),
        cost_estimate=pl.CostEstimate(flops=flops, bytes_accessed=moved, transcendentals=0),
    )(*args)


def parity_groups():
    pairs = lax.axis_size("dp") // INNER // 2
    return [
        [(2 * j + p) * INNER + z for j in range(pairs) for z in range(INNER)] for p in range(2)
    ]


def group_swap(blocks):
    return lax.all_to_all(
        blocks, "dp", split_axis=0, concat_axis=0, axis_index_groups=parity_groups(), tiled=True
    )


def neighbour_swap(block, side):
    count = lax.axis_size("dp")
    ring = count // INNER

    def other(y):
        return y ^ 1 if side == 0 else (y + 1 if y % 2 else y - 1) % ring

    pairs = [(d, other(d // INNER) * INNER + d % INNER) for d in range(count)]
    return lax.ppermute(block, "dp", pairs)


def expert_swap(rows):
    count = lax.axis_size("expert")
    got = lax.all_to_all(
        rows.reshape(count, CAP, rows.shape[1]),
        "expert",
        split_axis=0,
        concat_axis=0,
        tiled=True,
    )
    return got.reshape(rows.shape)


def local(tokens, routes, scores, w_gate, w_up, w_down, cotangent):
    tok_count, width = tokens.shape
    slots = EXPERTS * CAP
    pitch = pitch_of(width)
    group = lax.axis_size("dp") // 2
    each = HID // lax.axis_size("dp")
    half = HID // 2
    odd = lax.rem(lax.axis_index("dp") // INNER, 2).astype(jnp.int32).reshape(1)
    work = 6 * slots * HID * width

    sent, mix = run(
        pick_kernel,
        [((slots, 2 * pitch), BF16), ((4 * tok_count, slots), BF16)],
        (routes.T, scores.T, tokens, cotangent),
        4 * slots * tok_count * width,
        grant=None,
    )
    sent, odd = lax.optimization_barrier((sent, odd))
    rows = expert_swap(sent)
    cols = rows.shape[0]
    def columns(start):
        return tuple(
            lax.dynamic_slice_in_dim(w[0], start, half, axis=1) for w in (w_gate, w_up, w_down)
        )

    mine = columns(odd[0] * half)
    theirs = neighbour_swap(jnp.stack(columns((1 - odd[0]) * half)), 0)
    theirs = (theirs[0], theirs[1], theirs[2])
    pair_rows = neighbour_swap(rows, 0)
    shape = (group, 3 * each, cols)
    (share,) = run(row_kernel(False), [(shape, F32)], (rows,) + mine, work // 2)
    (pair_sums,) = run(row_kernel(True), [(shape, BF16)], (pair_rows,) + theirs + (share,), work // 2)
    own = jnp.sum(group_swap(pair_sums).astype(F32), axis=0)
    pre_gate, pre_up, grad_hidden = own[:each], own[each : 2 * each], own[2 * each :]
    sigma = jax.nn.sigmoid(pre_gate)
    active = pre_gate * sigma
    block = jnp.concatenate(
        [
            active * pre_up,
            grad_hidden * pre_up * sigma * (1.0 + pre_gate * (1.0 - sigma)),
            grad_hidden * active,
        ],
        axis=0,
    ).astype(BF16)
    near = group_swap(jnp.broadcast_to(block[None], (group,) + block.shape))
    outs_shape = (cols, 2 * pitch)
    (sent,) = run(out_kernel, [(outs_shape, BF16)], (near,) + theirs, work // 2)
    got = neighbour_swap(sent, 0)
    (outs,) = run(out_kernel, [(outs_shape, F32)], (near,) + mine, work // 2)
    outs = (outs + got.astype(F32)).astype(BF16)
    outs, late = lax.optimization_barrier((outs, near))
    far = tuple(
        neighbour_swap(late[side * group // 2 : (side + 1) * group // 2], side) for side in range(2)
    )
    home = expert_swap(outs)
    grads = run(grad_kernel, [((width, HID), BF16)] * 3, (odd, near) + far + (rows,), work)
    layer_out, grad_tokens = run(
        combine_kernel,
        [((tok_count, width), BF16)] * 2,
        (home, mix),
        16 * slots * tok_count * width,
    )
    return (layer_out, grad_tokens) + tuple(g[None] for g in grads)


def solution(mesh):
    rows = P("expert", "dp")
    table = P("expert", None)
    weight = P("expert", "dp", None)
    return jax.shard_map(
        local,
        mesh=mesh,
        in_specs=(rows, table, table, weight, weight, weight, rows),
        out_specs=(rows, rows, weight, weight, weight),
        check_vma=False,
    )
```

```python
import jax
import jax.numpy as jnp
from jax import lax
from jax.experimental import pallas as pl
from jax.experimental.pallas import tpu as pltpu
from jax.sharding import PartitionSpec as P

HID = 1024
EXPERTS = 32
CAP = 8
BF16 = jnp.bfloat16
F32 = jnp.float32
INNER = 4
LANES = 128

route_scale = 2.5


def pitch_of(width):
    return -(-width // LANES) * LANES


def flip(block):
    return block.astype(F32).T.astype(BF16)


def pick_kernel(routes_ref, scores_ref, tokens_ref, cotangent_ref, sent_ref, mix_ref):
    top_count, tok_count = routes_ref.shape
    slots = sent_ref.shape[0]
    width = tokens_ref.shape[1]
    pitch = sent_ref.shape[1] // 2
    scores = scores_ref[...].T
    gates = route_scale * scores / jnp.sum(scores, axis=1, keepdims=True)
    routes = routes_ref[...].astype(F32).T.astype(jnp.int32)
    slot = lax.broadcasted_iota(jnp.int32, (tok_count, slots), 1)
    shift = CAP.bit_length() - 1
    expert, rank = slot >> shift, slot & (CAP - 1)
    hit = jnp.zeros((tok_count, slots), F32)
    gate = jnp.zeros((tok_count, slots), F32)
    for k in range(top_count):
        same = routes[:, k : k + 1] == expert
        hit = hit + jnp.where(same, 1.0, 0.0)
        gate = gate + jnp.where(same, gates[:, k : k + 1], 0.0)
    row = lax.broadcasted_iota(jnp.int32, (tok_count, tok_count), 0)
    col = lax.broadcasted_iota(jnp.int32, (tok_count, tok_count), 1)
    earlier = jnp.where(col < row, 1.0, 0.0).astype(BF16)
    before = jnp.dot(earlier, hit.astype(BF16), preferred_element_type=F32)
    pick = jnp.where(before == rank.astype(F32), hit, 0.0)
    mix = pick * gate
    high = mix.astype(BF16)
    rest = mix - high.astype(F32)
    middle = rest.astype(BF16)
    low = (rest - middle.astype(F32)).astype(BF16)
    for index, term in enumerate((pick.astype(BF16), high, middle, low)):
        mix_ref[index * tok_count : (index + 1) * tok_count, :] = term
    picker = pick.T.astype(BF16)
    slot_gate = jnp.sum(mix.T, axis=1, keepdims=True)
    sent_ref[...] = jnp.zeros(sent_ref.shape, BF16)
    rows = jnp.dot(picker, tokens_ref[...], preferred_element_type=F32)
    sent_ref[:, :width] = rows.astype(BF16)
    rows = jnp.dot(picker, cotangent_ref[...], preferred_element_type=F32)
    sent_ref[:, pitch : pitch + width] = (rows * slot_gate).astype(BF16)


def row_kernel(base):
    def kernel(rows_ref, gate_ref, up_ref, down_ref, *refs):
        to_ref = refs[-1]
        width, span = gate_ref.shape
        pitch = rows_ref.shape[1] // 2
        group, depth, cols = to_ref.shape
        each = depth // 3
        x = flip(rows_ref[:, :width])
        do = flip(rows_ref[:, pitch : pitch + width])
        for index, (w_ref, r) in enumerate(((gate_ref, x), (up_ref, x), (down_ref, do))):
            part = lax.dot_general(
                w_ref[...], r, (((0,), (0,)), ((), ())), preferred_element_type=F32
            ).reshape(group, each, cols)
            at = pl.ds(index * each, each)
            if base:
                part = part + refs[0][:, at, :]
            to_ref[:, at, :] = part.astype(to_ref.dtype)

    return kernel


def array_rows(ref, index):
    group, depth, cols = ref.shape
    each = depth // 3
    return ref[:, index * each : (index + 1) * each, :].reshape(group * each, cols)


def out_kernel(near_ref, gate_ref, up_ref, down_ref, outs_ref):
    width = gate_ref.shape[0]
    pitch = outs_ref.shape[1] // 2

    def times(w_ref, index):
        return jnp.dot(w_ref[...], array_rows(near_ref, index), preferred_element_type=F32)

    out = times(down_ref, 0)
    grad = times(gate_ref, 1) + times(up_ref, 2)
    outs_ref[...] = jnp.zeros(outs_ref.shape, outs_ref.dtype)
    outs_ref[:, :width] = out.T.astype(outs_ref.dtype)
    outs_ref[:, pitch : pitch + width] = grad.T.astype(outs_ref.dtype)


def grad_kernel(odd_ref, near_ref, far0_ref, far1_ref, rows_ref, gate_ref, up_ref, down_ref):
    odd = odd_ref[0]
    width = gate_ref.shape[0]
    pitch = rows_ref.shape[1] // 2
    half = gate_ref.shape[1] // 2
    x = flip(rows_ref[:, :width])
    do = flip(rows_ref[:, pitch : pitch + width])
    places = ((near_ref, odd * half), (far0_ref, (1 - odd) * half))
    places += ((far1_ref, (1 - odd) * half + half // 2),)
    for ref, start in places:
        for to_ref, r, index in ((gate_ref, x, 1), (up_ref, x, 2), (down_ref, do, 0)):
            block = array_rows(ref, index)
            span = block.shape[0]
            to_ref[:, pl.ds(pl.multiple_of(start, half // 2), span)] = lax.dot_general(
                r, block, (((1,), (1,)), ((), ())), preferred_element_type=F32
            ).astype(BF16)


def combine_kernel(home_ref, mix_ref, out_ref, grad_ref):
    rows, width = out_ref.shape
    pitch = home_ref.shape[1] // 2
    sums = jnp.dot(mix_ref[...], home_ref[...], preferred_element_type=F32)
    gated = sums[rows : 2 * rows] + sums[2 * rows : 3 * rows] + sums[3 * rows :]
    out_ref[...] = gated[:, :width].astype(BF16)
    grad_ref[...] = sums[:rows, pitch : pitch + width].astype(BF16)


VMEM = pl.BlockSpec(memory_space=pltpu.VMEM)
SMEM = pl.BlockSpec(memory_space=pltpu.SMEM)


def run(kernel, outs, args, flops, grant=16):
    outs = [jax.ShapeDtypeStruct(shape, dtype) for shape, dtype in outs]
    moved = sum(a.size * a.dtype.itemsize for a in list(args) + outs)
    return pl.pallas_call(
        kernel,
        out_shape=outs,
        in_specs=[SMEM if a.shape == (1,) else VMEM for a in args],
        out_specs=[VMEM] * len(outs),
        compiler_params=pltpu.CompilerParams(vmem_limit_bytes=grant and grant * 2**20),
        cost_estimate=pl.CostEstimate(flops=flops, bytes_accessed=moved, transcendentals=0),
    )(*args)


def parity_groups():
    pairs = lax.axis_size("dp") // INNER // 2
    return [
        [(2 * j + p) * INNER + z for j in range(pairs) for z in range(INNER)] for p in range(2)
    ]


def group_swap(blocks):
    return lax.all_to_all(
        blocks, "dp", split_axis=0, concat_axis=0, axis_index_groups=parity_groups(), tiled=True
    )


def neighbour_swap(block, side):
    count = lax.axis_size("dp")
    ring = count // INNER

    def other(y):
        return y ^ 1 if side == 0 else (y + 1 if y % 2 else y - 1) % ring

    pairs = [(d, other(d // INNER) * INNER + d % INNER) for d in range(count)]
    return lax.ppermute(block, "dp", pairs)


def expert_swap(rows):
    count = lax.axis_size("expert")
    got = lax.all_to_all(
        rows.reshape(count, CAP, rows.shape[1]),
        "expert",
        split_axis=0,
        concat_axis=0,
        tiled=True,
    )
    return got.reshape(rows.shape)


def local(tokens, routes, scores, w_gate, w_up, w_down, cotangent):
    tok_count, width = tokens.shape
    slots = EXPERTS * CAP
    pitch = pitch_of(width)
    group = lax.axis_size("dp") // 2
    each = HID // lax.axis_size("dp")
    half = HID // 2
    odd = lax.rem(lax.axis_index("dp") // INNER, 2).astype(jnp.int32).reshape(1)
    work = 6 * slots * HID * width

    sent, mix = run(
        pick_kernel,
        [((slots, 2 * pitch), BF16), ((4 * tok_count, slots), BF16)],
        (routes.T, scores.T, tokens, cotangent),
        4 * slots * tok_count * width,
        grant=None,
    )
    sent, odd = lax.optimization_barrier((sent, odd))
    rows = expert_swap(sent)
    cols = rows.shape[0]
    def columns(start):
        return tuple(
            lax.dynamic_slice_in_dim(w[0], start, half, axis=1) for w in (w_gate, w_up, w_down)
        )

    mine = columns(odd[0] * half)
    theirs = tuple(neighbour_swap(w, 0) for w in columns((1 - odd[0]) * half))
    rows, theirs = lax.optimization_barrier((rows, theirs))
    pair_rows = neighbour_swap(rows, 0)
    shape = (group, 3 * each, cols)
    (share,) = run(row_kernel(False), [(shape, F32)], (rows,) + mine, work // 2)
    (pair_sums,) = run(row_kernel(True), [(shape, BF16)], (pair_rows,) + theirs + (share,), work // 2)
    own = jnp.sum(group_swap(pair_sums).astype(F32), axis=0)
    pre_gate, pre_up, grad_hidden = own[:each], own[each : 2 * each], own[2 * each :]
    sigma = jax.nn.sigmoid(pre_gate)
    active = pre_gate * sigma
    block = jnp.concatenate(
        [
            active * pre_up,
            grad_hidden * pre_up * sigma * (1.0 + pre_gate * (1.0 - sigma)),
            grad_hidden * active,
        ],
        axis=0,
    ).astype(BF16)
    near = group_swap(jnp.broadcast_to(block[None], (group,) + block.shape))
    outs_shape = (cols, 2 * pitch)
    (sent,) = run(out_kernel, [(outs_shape, BF16)], (near,) + theirs, work // 2)
    got = neighbour_swap(sent, 0)
    (outs,) = run(out_kernel, [(outs_shape, F32)], (near,) + mine, work // 2)
    outs = (outs + got.astype(F32)).astype(BF16)
    outs, late = lax.optimization_barrier((outs, near))
    far = tuple(
        neighbour_swap(late[side * group // 2 : (side + 1) * group // 2], side) for side in range(2)
    )
    home = expert_swap(outs)
    grads = run(grad_kernel, [((width, HID), BF16)] * 3, (odd, near) + far + (rows,), work)
    layer_out, grad_tokens = run(
        combine_kernel,
        [((tok_count, width), BF16)] * 2,
        (home, mix),
        16 * slots * tok_count * width,
    )
    return (layer_out, grad_tokens) + tuple(g[None] for g in grads)


def solution(mesh):
    rows = P("expert", "dp")
    table = P("expert", None)
    weight = P("expert", "dp", None)
    return jax.shard_map(
        local,
        mesh=mesh,
        in_specs=(rows, table, table, weight, weight, weight, rows),
        out_specs=(rows, rows, weight, weight, weight),
        check_vma=False,
    )
```

```python
import jax
import jax.numpy as jnp
from jax import lax
from jax.experimental import pallas as pl
from jax.experimental.pallas import tpu as pltpu
from jax.sharding import PartitionSpec as P

HID = 1024
EXPERTS = 32
CAP = 8
BF16 = jnp.bfloat16
F32 = jnp.float32
INNER = 4
LANES = 128

route_scale = 2.5


def pitch_of(width):
    return -(-width // LANES) * LANES


def flip(block):
    return block.astype(F32).T.astype(BF16)


def pick_kernel(odd_ref, routes_ref, scores_ref, tokens_ref, cotangent_ref, *refs):
    weights, (sent_ref, mix_ref), mine, theirs = refs[:3], refs[3:5], refs[5:8], refs[8:11]
    copies = list(column_copies(odd_ref[0], weights, mine, theirs, refs[11]))
    for copy in copies:
        copy.start()
    top_count, tok_count = routes_ref.shape
    slots = sent_ref.shape[0]
    width = tokens_ref.shape[1]
    pitch = sent_ref.shape[1] // 2
    scores = scores_ref[...].T
    gates = route_scale * scores / jnp.sum(scores, axis=1, keepdims=True)
    routes = routes_ref[...].astype(F32).T.astype(jnp.int32)
    slot = lax.broadcasted_iota(jnp.int32, (tok_count, slots), 1)
    shift = CAP.bit_length() - 1
    expert, rank = slot >> shift, slot & (CAP - 1)
    hit = jnp.zeros((tok_count, slots), F32)
    gate = jnp.zeros((tok_count, slots), F32)
    for k in range(top_count):
        same = routes[:, k : k + 1] == expert
        hit = hit + jnp.where(same, 1.0, 0.0)
        gate = gate + jnp.where(same, gates[:, k : k + 1], 0.0)
    row = lax.broadcasted_iota(jnp.int32, (tok_count, tok_count), 0)
    col = lax.broadcasted_iota(jnp.int32, (tok_count, tok_count), 1)
    earlier = jnp.where(col < row, 1.0, 0.0).astype(BF16)
    before = jnp.dot(earlier, hit.astype(BF16), preferred_element_type=F32)
    pick = jnp.where(before == rank.astype(F32), hit, 0.0)
    mix = pick * gate
    high = mix.astype(BF16)
    rest = mix - high.astype(F32)
    middle = rest.astype(BF16)
    low = (rest - middle.astype(F32)).astype(BF16)
    for index, term in enumerate((pick.astype(BF16), high, middle, low)):
        mix_ref[index * tok_count : (index + 1) * tok_count, :] = term
    picker = pick.T.astype(BF16)
    slot_gate = jnp.sum(mix.T, axis=1, keepdims=True)
    sent_ref[...] = jnp.zeros(sent_ref.shape, BF16)
    rows = jnp.dot(picker, tokens_ref[...], preferred_element_type=F32)
    sent_ref[:, :width] = rows.astype(BF16)
    rows = jnp.dot(picker, cotangent_ref[...], preferred_element_type=F32)
    sent_ref[:, pitch : pitch + width] = (rows * slot_gate).astype(BF16)
    for copy in copies:
        copy.wait()


def column_copies(odd, weights, mine, theirs, sems):
    half = mine[0].shape[1]
    for index, w_ref in enumerate(weights):
        for side, to_refs in enumerate((theirs, mine)):
            parity = odd if side else 1 - odd
            at = pl.ds(pl.multiple_of(parity * half, half), half)
            yield pltpu.make_async_copy(
                w_ref.at[:, at], to_refs[index], sems.at[2 * index + side]
            )


def row_kernel(base):
    def kernel(rows_ref, weights_ref, *refs):
        to_ref = refs[-1]
        width = weights_ref.shape[1]
        pitch = rows_ref.shape[1] // 2
        group, depth, cols = to_ref.shape
        each = depth // 3
        x = flip(rows_ref[:, :width])
        do = flip(rows_ref[:, pitch : pitch + width])
        for index, r in enumerate((x, x, do)):
            part = lax.dot_general(
                weights_ref[index], r, (((0,), (0,)), ((), ())), preferred_element_type=F32
            ).reshape(group, each, cols)
            at = pl.ds(index * each, each)
            if base:
                part = part + refs[0][:, at, :]
            to_ref[:, at, :] = part.astype(to_ref.dtype)

    return kernel


def array_rows(ref, index):
    group, depth, cols = ref.shape
    each = depth // 3
    return ref[:, index * each : (index + 1) * each, :].reshape(group * each, cols)


def out_kernel(near_ref, weights_ref, outs_ref):
    width = weights_ref.shape[1]
    pitch = outs_ref.shape[1] // 2

    def times(weight, index):
        rows = array_rows(near_ref, index)
        return jnp.dot(weights_ref[weight], rows, preferred_element_type=F32)

    out = times(2, 0)
    grad = times(0, 1) + times(1, 2)
    outs_ref[...] = jnp.zeros(outs_ref.shape, outs_ref.dtype)
    outs_ref[:, :width] = out.T.astype(outs_ref.dtype)
    outs_ref[:, pitch : pitch + width] = grad.T.astype(outs_ref.dtype)


def grad_kernel(odd_ref, near_ref, far0_ref, far1_ref, rows_ref, gate_ref, up_ref, down_ref):
    odd = odd_ref[0]
    width = gate_ref.shape[0]
    pitch = rows_ref.shape[1] // 2
    half = gate_ref.shape[1] // 2
    x = flip(rows_ref[:, :width])
    do = flip(rows_ref[:, pitch : pitch + width])
    places = ((near_ref, odd * half), (far0_ref, (1 - odd) * half))
    places += ((far1_ref, (1 - odd) * half + half // 2),)
    for ref, start in places:
        for to_ref, r, index in ((gate_ref, x, 1), (up_ref, x, 2), (down_ref, do, 0)):
            block = array_rows(ref, index)
            span = block.shape[0]
            to_ref[:, pl.ds(pl.multiple_of(start, half // 2), span)] = lax.dot_general(
                r, block, (((1,), (1,)), ((), ())), preferred_element_type=F32
            ).astype(BF16)


def combine_kernel(home_ref, mix_ref, out_ref, grad_ref):
    rows, width = out_ref.shape
    pitch = home_ref.shape[1] // 2
    sums = jnp.dot(mix_ref[...], home_ref[...], preferred_element_type=F32)
    gated = sums[rows : 2 * rows] + sums[2 * rows : 3 * rows] + sums[3 * rows :]
    out_ref[...] = gated[:, :width].astype(BF16)
    grad_ref[...] = sums[:rows, pitch : pitch + width].astype(BF16)


VMEM = pl.BlockSpec(memory_space=pltpu.VMEM)
SMEM = pl.BlockSpec(memory_space=pltpu.SMEM)


def run(kernel, outs, args, flops):
    outs = [jax.ShapeDtypeStruct(shape, dtype) for shape, dtype in outs]
    moved = sum(a.size * a.dtype.itemsize for a in list(args) + outs)
    return pl.pallas_call(
        kernel,
        out_shape=outs,
        in_specs=[SMEM if a.shape == (1,) else VMEM for a in args],
        out_specs=[VMEM] * len(outs),
        compiler_params=pltpu.CompilerParams(vmem_limit_bytes=16 * 2**20),
        cost_estimate=pl.CostEstimate(flops=flops, bytes_accessed=moved, transcendentals=0),
    )(*args)


def parity_groups():
    pairs = lax.axis_size("dp") // INNER // 2
    return [
        [(2 * j + p) * INNER + z for j in range(pairs) for z in range(INNER)] for p in range(2)
    ]


def group_swap(blocks):
    return lax.all_to_all(
        blocks, "dp", split_axis=0, concat_axis=0, axis_index_groups=parity_groups(), tiled=True
    )


def neighbour_swap(block, side):
    count = lax.axis_size("dp")
    ring = count // INNER

    def other(y):
        return y ^ 1 if side == 0 else (y + 1 if y % 2 else y - 1) % ring

    pairs = [(d, other(d // INNER) * INNER + d % INNER) for d in range(count)]
    return lax.ppermute(block, "dp", pairs)


def expert_swap(rows):
    count = lax.axis_size("expert")
    got = lax.all_to_all(
        rows.reshape(count, CAP, rows.shape[1]),
        "expert",
        split_axis=0,
        concat_axis=0,
        tiled=True,
    )
    return got.reshape(rows.shape)


def local(tokens, routes, scores, w_gate, w_up, w_down, cotangent):
    tok_count, width = tokens.shape
    slots = EXPERTS * CAP
    pitch = pitch_of(width)
    group = lax.axis_size("dp") // 2
    each = HID // lax.axis_size("dp")
    half = HID // 2
    odd = lax.rem(lax.axis_index("dp") // INNER, 2).astype(jnp.int32).reshape(1)
    work = 6 * slots * HID * width

    place = pl.BlockSpec(memory_space=pl.ANY)
    shapes = ((slots, 2 * pitch), (4 * tok_count, slots)) + ((width, half),) * 6
    sent, mix, *split = pl.pallas_call(
        pick_kernel,
        out_shape=[jax.ShapeDtypeStruct(dims, BF16) for dims in shapes],
        in_specs=[SMEM] + [VMEM] * 4 + [place] * 3,
        out_specs=[VMEM] * 2 + [place] * 6,
        scratch_shapes=[pltpu.SemaphoreType.DMA((6,))],
    )(odd, routes.T, scores.T, tokens, cotangent, w_gate[0], w_up[0], w_down[0])
    mine = jnp.stack(split[:3])
    theirs = neighbour_swap(jnp.stack(split[3:]), 0)
    rows = expert_swap(sent)
    cols = rows.shape[0]
    pair_rows = neighbour_swap(rows, 0)
    shape = (group, 3 * each, cols)
    (share,) = run(row_kernel(False), [(shape, F32)], (rows, mine), work // 2)
    (pair_sums,) = run(row_kernel(True), [(shape, BF16)], (pair_rows, theirs, share), work // 2)
    own = jnp.sum(group_swap(pair_sums).astype(F32), axis=0)
    pre_gate, pre_up, grad_hidden = own[:each], own[each : 2 * each], own[2 * each :]
    sigma = jax.nn.sigmoid(pre_gate)
    active = pre_gate * sigma
    block = jnp.concatenate(
        [
            active * pre_up,
            grad_hidden * pre_up * sigma * (1.0 + pre_gate * (1.0 - sigma)),
            grad_hidden * active,
        ],
        axis=0,
    ).astype(BF16)
    near = group_swap(jnp.broadcast_to(block[None], (group,) + block.shape))
    outs_shape = (cols, 2 * pitch)
    (sent,) = run(out_kernel, [(outs_shape, BF16)], (near, theirs), work // 2)
    got = neighbour_swap(sent, 0)
    (outs,) = run(out_kernel, [(outs_shape, F32)], (near, mine), work // 2)
    outs = (outs + got.astype(F32)).astype(BF16)
    outs, late = lax.optimization_barrier((outs, near))
    far = tuple(
        neighbour_swap(late[side * group // 2 : (side + 1) * group // 2], side) for side in range(2)
    )
    home = expert_swap(outs)
    grads = run(grad_kernel, [((width, HID), BF16)] * 3, (odd, near) + far + (rows,), work)
    layer_out, grad_tokens = run(
        combine_kernel,
        [((tok_count, width), BF16)] * 2,
        (home, mix),
        16 * slots * tok_count * width,
    )
    return (layer_out, grad_tokens) + tuple(g[None] for g in grads)


def solution(mesh):
    rows = P("expert", "dp")
    table = P("expert", None)
    weight = P("expert", "dp", None)
    return jax.shard_map(
        local,
        mesh=mesh,
        in_specs=(rows, table, table, weight, weight, weight, rows),
        out_specs=(rows, rows, weight, weight, weight),
        check_vma=False,
    )
```

```python
import jax
import jax.numpy as jnp
from jax import lax
from jax.experimental import pallas as pl
from jax.experimental.pallas import tpu as pltpu
from jax.sharding import PartitionSpec as P

HID = 1024
EXPERTS = 32
CAP = 8
BF16 = jnp.bfloat16
F32 = jnp.float32
INNER = 4
LANES = 128

route_scale = 2.5


def pitch_of(width):
    return -(-width // LANES) * LANES


def flip(block):
    return block.astype(F32).T.astype(BF16)


def pick_kernel(routes_ref, scores_ref, tokens_ref, cotangent_ref, sent_ref, mix_ref):
    top_count, tok_count = routes_ref.shape
    slots = sent_ref.shape[0]
    width = tokens_ref.shape[1]
    pitch = sent_ref.shape[1] // 2
    scores = scores_ref[...].T
    gates = route_scale * scores / jnp.sum(scores, axis=1, keepdims=True)
    routes = routes_ref[...].astype(F32).T.astype(jnp.int32)
    slot = lax.broadcasted_iota(jnp.int32, (tok_count, slots), 1)
    shift = CAP.bit_length() - 1
    expert, rank = slot >> shift, slot & (CAP - 1)
    hit = jnp.zeros((tok_count, slots), F32)
    gate = jnp.zeros((tok_count, slots), F32)
    for k in range(top_count):
        same = routes[:, k : k + 1] == expert
        hit = hit + jnp.where(same, 1.0, 0.0)
        gate = gate + jnp.where(same, gates[:, k : k + 1], 0.0)
    row = lax.broadcasted_iota(jnp.int32, (tok_count, tok_count), 0)
    col = lax.broadcasted_iota(jnp.int32, (tok_count, tok_count), 1)
    earlier = jnp.where(col < row, 1.0, 0.0).astype(BF16)
    before = jnp.dot(earlier, hit.astype(BF16), preferred_element_type=F32)
    pick = jnp.where(before == rank.astype(F32), hit, 0.0)
    mix = pick * gate
    high = mix.astype(BF16)
    rest = mix - high.astype(F32)
    middle = rest.astype(BF16)
    low = (rest - middle.astype(F32)).astype(BF16)
    for index, term in enumerate((pick.astype(BF16), high, middle, low)):
        mix_ref[index * tok_count : (index + 1) * tok_count, :] = term
    picker = pick.T.astype(BF16)
    slot_gate = jnp.sum(mix.T, axis=1, keepdims=True)
    sent_ref[...] = jnp.zeros(sent_ref.shape, BF16)
    rows = jnp.dot(picker, tokens_ref[...], preferred_element_type=F32)
    sent_ref[:, :width] = rows.astype(BF16)
    rows = jnp.dot(picker, cotangent_ref[...], preferred_element_type=F32)
    sent_ref[:, pitch : pitch + width] = (rows * slot_gate).astype(BF16)


def row_kernel(base):
    def kernel(rows_ref, gate_ref, up_ref, down_ref, *refs):
        to_ref = refs[-1]
        width, span = gate_ref.shape
        pitch = rows_ref.shape[1] // 2
        group, depth, cols = to_ref.shape
        each = depth // 3
        x = flip(rows_ref[:, :width])
        do = flip(rows_ref[:, pitch : pitch + width])
        for index, (w_ref, r) in enumerate(((gate_ref, x), (up_ref, x), (down_ref, do))):
            part = lax.dot_general(
                w_ref[...], r, (((0,), (0,)), ((), ())), preferred_element_type=F32
            ).reshape(group, each, cols)
            at = pl.ds(index * each, each)
            if base:
                part = part + refs[0][:, at, :]
            to_ref[:, at, :] = part.astype(to_ref.dtype)

    return kernel


def array_rows(ref, index):
    group, depth, cols = ref.shape
    each = depth // 3
    return ref[:, index * each : (index + 1) * each, :].reshape(group * each, cols)


def out_kernel(near_ref, gate_ref, up_ref, down_ref, outs_ref):
    width = gate_ref.shape[0]
    pitch = outs_ref.shape[1] // 2

    def times(w_ref, index):
        return jnp.dot(w_ref[...], array_rows(near_ref, index), preferred_element_type=F32)

    out = times(down_ref, 0)
    grad = times(gate_ref, 1) + times(up_ref, 2)
    outs_ref[...] = jnp.zeros(outs_ref.shape, outs_ref.dtype)
    outs_ref[:, :width] = out.T.astype(outs_ref.dtype)
    outs_ref[:, pitch : pitch + width] = grad.T.astype(outs_ref.dtype)


def outer_products(rows_ref, width, ref):
    pitch = rows_ref.shape[1] // 2
    x = flip(rows_ref[:, :width])
    do = flip(rows_ref[:, pitch : pitch + width])
    for r, index in ((x, 1), (x, 2), (do, 0)):
        yield lax.dot_general(
            r, array_rows(ref, index), (((1,), (1,)), ((), ())), preferred_element_type=F32
        ).astype(BF16)


def near_grad_kernel(near_ref, rows_ref, *to_refs):
    for to_ref, block in zip(to_refs, outer_products(rows_ref, to_refs[0].shape[0], near_ref)):
        to_ref[...] = block


def grad_kernel(odd_ref, far0_ref, far1_ref, rows_ref, *refs):
    odd = odd_ref[0]
    nears, to_refs = refs[:3], refs[3:]
    width, half = nears[0].shape
    for near_ref, to_ref in zip(nears, to_refs):
        to_ref[:, pl.ds(pl.multiple_of(odd * half, half), half)] = near_ref[...]
    for side, ref in enumerate((far0_ref, far1_ref)):
        start = pl.multiple_of((1 - odd) * half + side * (half // 2), half // 2)
        for to_ref, block in zip(to_refs, outer_products(rows_ref, width, ref)):
            to_ref[:, pl.ds(start, half // 2)] = block


def combine_kernel(home_ref, mix_ref, out_ref, grad_ref):
    rows, width = out_ref.shape
    pitch = home_ref.shape[1] // 2
    sums = jnp.dot(mix_ref[...], home_ref[...], preferred_element_type=F32)
    gated = sums[rows : 2 * rows] + sums[2 * rows : 3 * rows] + sums[3 * rows :]
    out_ref[...] = gated[:, :width].astype(BF16)
    grad_ref[...] = sums[:rows, pitch : pitch + width].astype(BF16)


VMEM = pl.BlockSpec(memory_space=pltpu.VMEM)
SMEM = pl.BlockSpec(memory_space=pltpu.SMEM)


def run(kernel, outs, args, flops, grant=16):
    outs = [jax.ShapeDtypeStruct(shape, dtype) for shape, dtype in outs]
    moved = sum(a.size * a.dtype.itemsize for a in list(args) + outs)
    return pl.pallas_call(
        kernel,
        out_shape=outs,
        in_specs=[SMEM if a.shape == (1,) else VMEM for a in args],
        out_specs=[VMEM] * len(outs),
        compiler_params=pltpu.CompilerParams(vmem_limit_bytes=grant and grant * 2**20),
        cost_estimate=pl.CostEstimate(flops=flops, bytes_accessed=moved, transcendentals=0),
    )(*args)


def parity_groups():
    pairs = lax.axis_size("dp") // INNER // 2
    return [
        [(2 * j + p) * INNER + z for j in range(pairs) for z in range(INNER)] for p in range(2)
    ]


def group_swap(blocks):
    return lax.all_to_all(
        blocks, "dp", split_axis=0, concat_axis=0, axis_index_groups=parity_groups(), tiled=True
    )


def neighbour_swap(block, side):
    count = lax.axis_size("dp")
    ring = count // INNER

    def other(y):
        return y ^ 1 if side == 0 else (y + 1 if y % 2 else y - 1) % ring

    pairs = [(d, other(d // INNER) * INNER + d % INNER) for d in range(count)]
    return lax.ppermute(block, "dp", pairs)


def expert_swap(rows):
    count = lax.axis_size("expert")
    got = lax.all_to_all(
        rows.reshape(count, CAP, rows.shape[1]),
        "expert",
        split_axis=0,
        concat_axis=0,
        tiled=True,
    )
    return got.reshape(rows.shape)


def local(tokens, routes, scores, w_gate, w_up, w_down, cotangent):
    tok_count, width = tokens.shape
    slots = EXPERTS * CAP
    pitch = pitch_of(width)
    group = lax.axis_size("dp") // 2
    each = HID // lax.axis_size("dp")
    half = HID // 2
    odd = lax.rem(lax.axis_index("dp") // INNER, 2).astype(jnp.int32).reshape(1)
    work = 6 * slots * HID * width

    sent, mix = run(
        pick_kernel,
        [((slots, 2 * pitch), BF16), ((4 * tok_count, slots), BF16)],
        (routes.T, scores.T, tokens, cotangent),
        4 * slots * tok_count * width,
        grant=None,
    )
    sent, odd = lax.optimization_barrier((sent, odd))
    rows = expert_swap(sent)
    cols = rows.shape[0]
    def columns(start):
        return tuple(
            lax.dynamic_slice_in_dim(w[0], start, half, axis=1) for w in (w_gate, w_up, w_down)
        )

    mine = columns(odd[0] * half)
    theirs = neighbour_swap(jnp.stack(columns((1 - odd[0]) * half)), 0)
    theirs = (theirs[0], theirs[1], theirs[2])
    pair_rows = neighbour_swap(rows, 0)
    shape = (group, 3 * each, cols)
    (share,) = run(row_kernel(False), [(shape, F32)], (rows,) + mine, work // 2)
    (pair_sums,) = run(row_kernel(True), [(shape, BF16)], (pair_rows,) + theirs + (share,), work // 2)
    own = jnp.sum(group_swap(pair_sums).astype(F32), axis=0)
    pre_gate, pre_up, grad_hidden = own[:each], own[each : 2 * each], own[2 * each :]
    sigma = jax.nn.sigmoid(pre_gate)
    active = pre_gate * sigma
    block = jnp.concatenate(
        [
            active * pre_up,
            grad_hidden * pre_up * sigma * (1.0 + pre_gate * (1.0 - sigma)),
            grad_hidden * active,
        ],
        axis=0,
    ).astype(BF16)
    near = group_swap(jnp.broadcast_to(block[None], (group,) + block.shape))
    outs_shape = (cols, 2 * pitch)
    (sent,) = run(out_kernel, [(outs_shape, BF16)], (near,) + theirs, work // 2)
    got = neighbour_swap(sent, 0)
    (outs,) = run(out_kernel, [(outs_shape, F32)], (near,) + mine, work // 2)
    outs = (outs + got.astype(F32)).astype(BF16)
    outs, late = lax.optimization_barrier((outs, near))
    far = tuple(
        neighbour_swap(late[side * group // 2 : (side + 1) * group // 2], side) for side in range(2)
    )
    home = expert_swap(outs)
    nears = run(near_grad_kernel, [((width, half), BF16)] * 3, (late, rows), work // 2)
    grads = run(
        grad_kernel, [((width, HID), BF16)] * 3, (odd,) + far + (rows,) + tuple(nears), work // 2
    )
    layer_out, grad_tokens = run(
        combine_kernel,
        [((tok_count, width), BF16)] * 2,
        (home, mix),
        16 * slots * tok_count * width,
    )
    return (layer_out, grad_tokens) + tuple(g[None] for g in grads)


def solution(mesh):
    rows = P("expert", "dp")
    table = P("expert", None)
    weight = P("expert", "dp", None)
    return jax.shard_map(
        local,
        mesh=mesh,
        in_specs=(rows, table, table, weight, weight, weight, rows),
        out_specs=(rows, rows, weight, weight, weight),
        check_vma=False,
    )
```
